32 devices in a mesh: dp: 16 (over z, y, x), mp: 2 (over core).
Axes of the slice: x: 2, y: 2, z: 4, core: 2. Of those that a mesh axis runs over, the one named last changes fastest.
Arguments:
- tokens: bfloat16 [16, 1024, 768], P('dp', 'mp'), may hold values from -5 to 5
- segments: int32 [16, 1024], P('dp'), may hold values from 0 to 31, as said below
- cls_pos: int32 [16, 32], P('dp', 'mp'), may hold values from 0 to 1023, as said below
- keep_mask: int32 [16, 1024, 2, 2, 768], P('dp', 'mp'), may hold values 0 or 1
- cotangent: bfloat16 [16, 1024, 2, 768], P('dp', 'mp'), may hold values from -6 to 6
- contrast_loss_scale: float32 [], replicated, may hold values from 1024 to 4096
- q_weight: bfloat16 [768, 768], P(None, 'mp'), may hold values from -0.21875 to 0.21875
- q_bias: float32 [768], P('mp'), may hold values from -3 to 3
- k_weight: bfloat16 [768, 768], P(None, 'mp'), may hold values from -0.21875 to 0.21875
- v_weight: bfloat16 [768, 768], P(None, 'mp'), may hold values from -0.21875 to 0.21875
- v_bias: float32 [768], P('mp'), may hold values from -3 to 3
- o_weight: bfloat16 [768, 768], P('mp'), may hold values from -1.25 to 1.25
- o_bias: float32 [768], replicated, may hold values from -3 to 3
- norm1_gain: float32 [768], replicated, may hold values from 0.5 to 1.5
- norm1_shift: float32 [768], replicated, may hold values from -3 to 3
- up_weight: bfloat16 [768, 3072], P(None, 'mp'), may hold values from -0.21875 to 0.21875
- up_bias: float32 [3072], P('mp'), may hold values from -3 to 3
- down_weight: bfloat16 [3072, 768], P('mp'), may hold values from -0.15625 to 0.15625
- down_bias: float32 [768], replicated, may hold values from -3 to 3
- norm2_gain: float32 [768], replicated, may hold values from 0.5 to 1.5
- norm2_shift: float32 [768], replicated, may hold values from -3 to 3
- pooler_weight: bfloat16 [768, 768], replicated, may hold values from -0.21875 to 0.21875
- pool_bias: float32 [768], replicated, may hold values from -3 to 3
Outputs:
- contrastive_loss: float32 [], replicated
- layer_out: bfloat16 [16, 1024, 2, 768], P('dp', 'mp')
- grad_tokens: float32 [16, 1024, 768], P('dp', 'mp')
- grad_q_weight: float32 [768, 768], P('dp', 'mp')
- grad_q_bias: float32 [768], replicated
- grad_k_weight: float32 [768, 768], P('dp', 'mp')
- grad_v_weight: float32 [768, 768], P('dp', 'mp')
- grad_v_bias: float32 [768], replicated
- grad_o_weight: float32 [768, 768], P('mp', 'dp')
- grad_o_bias: float32 [768], replicated
- grad_norm1_gain: float32 [768], replicated
- grad_norm1_shift: float32 [768], replicated
- grad_up_weight: float32 [768, 3072], P('dp', 'mp')
- grad_up_bias: float32 [3072], replicated
- grad_down_weight: float32 [3072, 768], P('mp', 'dp')
- grad_down_bias: float32 [768], replicated
- grad_norm2_gain: float32 [768], replicated
- grad_norm2_shift: float32 [768], replicated
- grad_pool_weight: float32 [768, 768], P('mp', 'dp')
- grad_pool_bias: float32 [768], replicated
- alignment: float32 [], replicated
- uniformity: float32 [], replicated
The draws below stay inside these ranges and needn't reach their ends.
Inputs may be any that keep to these rules, and one draw needn't show every extreme that they name: `segments`: each row consists of 2 equal parts of 512 positions, each holding 32 / 2 whole sentences in order; segment numbers count a row's sentences from 0 and never fall; every sentence has 1 to 64 tokens and every part holds one of exactly 64. cls_pos[r, s] is the first position of sentence s of row r, as numbered in segments.
All inputs are finite; a program needn't handle non-finite values. No bound on the sum of `keep_mask` on one device may be relied on, other than what follows from the above.
Results may differ from the reference program's by a relative error of at most 0.02.
Values may be sent and summed in bfloat16 or wider, within the bound.
No kernel may reach another device: no remote copies, remote signals or barrier semaphores. Data moves between devices by JAX's collectives and lax.ppermute only.
A program may use at most 256 MiB of HBM per device.

```python
import math
import jax
import jax.numpy as jnp
from jax import lax

D = 768
HEADS = 12
FF = 3072
HEAD_DIM = 64
ROW_LEN = 1024
SENT = 32
ROWS_DEV = 1
ROWS = 16
NS = 512
ROW_PARTS = 2


def sentence_starts(key):
    per_part = SENT // ROW_PARTS
    mean_len = ROW_LEN // SENT
    base_key = jax.random.fold_in(key, 7)
    key_middle, key_pairs, key_order = jax.random.split(base_key, 3)
    middle = jax.random.randint(key_middle, (ROWS, ROW_PARTS, 1), 1, mean_len)
    pair_count = (per_part - 3) // 2
    shifts = jax.random.randint(key_pairs, (ROWS, ROW_PARTS, pair_count), 0, mean_len)
    pieces = [jnp.full((ROWS, ROW_PARTS, 1), 2 * mean_len, jnp.int32), middle, mean_len - middle, mean_len + shifts, mean_len - shifts]
    if (per_part - 3) % 2 == 1:
        pieces.append(jnp.full((ROWS, ROW_PARTS, 1), mean_len, jnp.int32))
    lengths = jnp.concatenate(pieces, axis=-1).astype(jnp.int32)
    ranks = jax.random.randint(key_order, (ROWS, ROW_PARTS, per_part), 0, 1 << 20) * per_part
    ranks = ranks + jnp.arange(per_part, dtype=jnp.int32)[None, None, :]
    order = jnp.argsort(ranks, axis=-1, stable=True)
    lengths = jnp.take_along_axis(lengths, order, axis=-1)
    part_base = jnp.arange(ROW_PARTS, dtype=jnp.int32)[None, :, None] * (ROW_LEN // ROW_PARTS)
    starts = jnp.cumsum(lengths, axis=-1) - lengths + part_base
    return starts.reshape(ROWS, SENT).astype(jnp.int32)


def segment_numbers(key):
    starts = sentence_starts(key)
    positions = jnp.arange(ROW_LEN, dtype=jnp.int32)
    begun = (starts[:, :, None] <= positions[None, None, :]).astype(jnp.int32)
    return (jnp.sum(begun, axis=1) - 1).astype(jnp.int32)


def draw_segments(key, part):
    return segment_numbers(key)


def draw_cls_pos(key, part):
    return sentence_starts(key)


def draw_tokens(key, part):
    segs = segment_numbers(key)
    base_key = jax.random.fold_in(key, 11)
    key_noise, key_far, key_pair, key_share = jax.random.split(base_key, 4)
    per_dev = SENT // ROW_PARTS
    dev_count = ROWS // ROWS_DEV * ROW_PARTS
    half_count = dev_count // 2
    slot_count = ROWS_DEV * per_dev
    row_ids = jnp.arange(ROWS, dtype=jnp.int32)[:, None]
    sent_ids = jnp.arange(SENT, dtype=jnp.int32)[None, :]
    device = row_ids // ROWS_DEV * ROW_PARTS + sent_ids // per_dev
    slot = row_ids % ROWS_DEV * per_dev + sent_ids % per_dev
    far_group = device % half_count * slot_count + slot
    pair_group = device // 2 * slot_count + slot
    even_slot = slot % 2 == 0
    far_table = jnp.clip(jax.random.normal(key_far, (half_count * slot_count, D), jnp.float32), -3.5, 3.5)
    pair_table = jnp.clip(jax.random.normal(key_pair, (half_count * slot_count, D), jnp.float32), -3.5, 3.5)
    noise = jnp.clip(jax.random.normal(key_noise, (ROWS, ROW_LEN, D), jnp.float32), -3.5, 3.5)
    share_far = jax.random.uniform(jax.random.fold_in(key_share, 1), (half_count * slot_count,), jnp.float32, 0.5, 0.95)
    share_pair = jax.random.uniform(jax.random.fold_in(key_share, 2), (half_count * slot_count,), jnp.float32, 0.5, 0.95)
    topic = jnp.where(even_slot[:, :, None], far_table[far_group], pair_table[pair_group])
    share = jnp.where(even_slot, share_far[far_group], share_pair[pair_group])
    topic_tok = jnp.take_along_axis(topic, segs[:, :, None], axis=1)
    share_tok = jnp.take_along_axis(share, segs, axis=1)[:, :, None]
    values = share_tok * topic_tok + jnp.sqrt(1.0 - share_tok * share_tok) * noise
    return values.astype(jnp.bfloat16)


def plant(entries, own_key, low, top_value):
    longest = entries.shape.index(max(entries.shape))
    spots = []
    for shift in (0, 1):
        where = [jax.random.randint(jax.random.fold_in(own_key, axis), (), 0, length) for axis, length in enumerate(entries.shape)]
        where[longest] = (where[longest] + shift) % entries.shape[longest]
        spots.append(tuple(where))
    return entries.at[spots[0]].set(low).at[spots[1]].set(top_value)


def levels(key, dims, shards, smallest, top_value):
    loudness, own = 1.0, jax.random.fold_in(key, 6)
    for position, parts in shards:
        draws = jnp.exp(jax.random.uniform(jax.random.fold_in(own, position), (parts,), jnp.float32, smallest / len(shards), top_value / len(shards)))
        loudness = loudness * jnp.repeat(draws, dims[position] // parts).reshape([-1 if axis == position else 1 for axis in range(len(dims))])
    return loudness


def bell_draw(rng, dims, scale, reach, shards=(), kind=jnp.bfloat16):
    values = scale * jax.random.normal(rng, dims, jnp.float32)
    if shards:
        values = values * levels(rng, dims, shards, -0.22, 0.18)
    return jnp.clip(values, -reach, reach).astype(kind)


def setup_inputs(seed: int = 0) -> dict:
    key_of = jax.random.split(jax.random.key(seed), 24)
    tokens = draw_tokens(jax.random.fold_in(key_of[23], 71), 0)
    segments = draw_segments(jax.random.fold_in(key_of[23], 71), 0)
    cls_pos = draw_cls_pos(jax.random.fold_in(key_of[23], 71), 0)
    keep_mask = plant((jax.random.randint(key_of[3], (ROWS, ROW_LEN, 2, 2, D), 0, 10) < 9).astype(jnp.int32), jax.random.fold_in(key_of[3], 1), 0, 1)
    cotangent = bell_draw(key_of[4], (ROWS, ROW_LEN, 2, D), 1.0, 6.0, ((0, 16), (1, 2)))
    contrast_loss_scale = jnp.clip(jnp.exp(jax.random.uniform(key_of[5], (), jnp.float32, math.log(1024.0), math.log(4096.0))), 1024.0, 4096.0)
    q_weight = bell_draw(key_of[6], (D, D), D ** -0.5, 0.21875, ((1, 2),))
    q_bias = bell_draw(key_of[7], (D,), 0.5, 3.0, ((0, 2),), jnp.float32)
    k_weight = bell_draw(key_of[8], (D, D), D ** -0.5, 0.21875, ((1, 2),))
    v_weight = bell_draw(key_of[9], (D, D), D ** -0.5, 0.21875, ((1, 2),))
    v_bias = bell_draw(key_of[10], (D,), 0.5, 3.0, ((0, 2),), jnp.float32)
    o_weight = bell_draw(key_of[11], (D, D), (D // 32) ** -0.5, 1.25, ((0, 2),))
    o_bias = bell_draw(key_of[12], (D,), 0.5, 3.0, (), jnp.float32)
    norm1_gain = jnp.clip(1.0 + 0.1 * jax.random.normal(key_of[13], (D,), jnp.float32), 0.5, 1.5)
    norm1_shift = bell_draw(key_of[14], (D,), 0.5, 3.0, (), jnp.float32)
    up_weight = bell_draw(key_of[15], (D, FF), D ** -0.5, 0.21875, ((1, 2),))
    up_bias = bell_draw(key_of[16], (FF,), 0.5, 3.0, ((0, 2),), jnp.float32)
    down_weight = bell_draw(key_of[17], (FF, D), (FF // 2) ** -0.5, 0.15625, ((0, 2),))
    down_bias = bell_draw(key_of[18], (D,), 0.5, 3.0, (), jnp.float32)
    norm2_gain = jnp.clip(1.0 + 0.1 * jax.random.normal(key_of[19], (D,), jnp.float32), 0.5, 1.5)
    norm2_shift = bell_draw(key_of[20], (D,), 0.5, 3.0, (), jnp.float32)
    pooler_weight = bell_draw(key_of[21], (D, D), D ** -0.5, 0.21875)
    pool_bias = bell_draw(key_of[22], (D,), 0.5, 3.0, (), jnp.float32)
    return {"tokens": tokens, "segments": segments, "cls_pos": cls_pos, "keep_mask": keep_mask, "cotangent": cotangent, "contrast_loss_scale": contrast_loss_scale, "q_weight": q_weight, "q_bias": q_bias, "k_weight": k_weight, "v_weight": v_weight, "v_bias": v_bias, "o_weight": o_weight, "o_bias": o_bias, "norm1_gain": norm1_gain, "norm1_shift": norm1_shift, "up_weight": up_weight, "up_bias": up_bias, "down_weight": down_weight, "down_bias": down_bias, "norm2_gain": norm2_gain, "norm2_shift": norm2_shift, "pooler_weight": pooler_weight, "pool_bias": pool_bias}


@jax.custom_vjp
def low(v):
    return lax.optimization_barrier(v.astype(jnp.bfloat16)).astype(jnp.float32)

@jax.custom_vjp
def low_back(v):
    return v

def low_keep(v):
    return (low(v), None)

def low_pass(kept, grad):
    return (grad,)

def back_keep(v):
    return (v, None)

def back_low(kept, grad):
    return (low(grad),)
low.defvjp(low_keep, low_pass)
low_back.defvjp(back_keep, back_low)
PRECISE = lax.Precision.HIGHEST
NORM_EPS = 1e-06
SOFTMAX_TEMP = 0.05
KEEP_SCALE = 10.0 / 9.0

def matmul_high(left, right):
    return jnp.matmul(left, right, precision=PRECISE)

def layer_norm(values, gain, shift):
    centre = values - lax.optimization_barrier(jnp.mean(values, axis=-1, keepdims=True))
    spread = lax.optimization_barrier(jnp.mean(centre * centre, axis=-1, keepdims=True))
    return centre * lax.rsqrt(spread + NORM_EPS) * gain + shift

def one_row(weights, tokens_row, keep_row, segment_row, cls_row):
    q_weight, q_bias, k_weight, v_weight, v_bias, o_weight, o_bias, norm1_gain, norm1_shift, up_weight, up_bias, down_weight, down_bias, norm2_gain, norm2_shift, pooler_weight, pool_bias = weights
    head_shape = (ROW_LEN, HEADS, HEAD_DIM)
    queries = low(low_back(matmul_high(tokens_row, q_weight) + q_bias)).reshape(head_shape)
    key_rows = low(low_back(matmul_high(tokens_row, k_weight))).reshape(head_shape)
    value_rows = low(low_back(matmul_high(tokens_row, v_weight) + v_bias)).reshape(head_shape)
    scores = jnp.einsum('qhd,khd->hqk', queries, key_rows, precision=PRECISE) * HEAD_DIM ** (-0.5)
    scores = low_back(scores)
    same_doc = segment_row[:, None] == segment_row[None, :]
    scores = jnp.where(same_doc[None], scores, -1e+30)
    prob_vals = low(jax.nn.softmax(scores, axis=-1))
    mixed_out = jnp.einsum('hqk,khd->qhd', prob_vals, value_rows, precision=PRECISE).reshape(ROW_LEN, D)
    mixed_out = low(low_back(mixed_out))
    attn_full = low_back(matmul_high(mixed_out, o_weight)) + o_bias
    keep_scaled = keep_row.astype(jnp.float32) * KEEP_SCALE
    pre_first = tokens_row[:, None, :] + keep_scaled[:, 0] * attn_full[:, None, :]
    hidden_in = layer_norm(pre_first, norm1_gain, norm1_shift)
    hidden_low = low(hidden_in)
    up_part = low_back(matmul_high(hidden_low, up_weight) + up_bias)
    activ = low(jax.nn.gelu(up_part, approximate=False))
    down_part = low_back(matmul_high(activ, down_weight)) + down_bias
    pre_second = hidden_in + keep_scaled[:, 1] * down_part
    row_out = low(layer_norm(pre_second, norm2_gain, norm2_shift))
    cls_rows = row_out[cls_row]
    pooled = low(jnp.tanh(low_back(matmul_high(cls_rows, pooler_weight) + pool_bias)))
    return (row_out, pooled)

def forward(weights, token_values, keep_mask, segments, cls_pos):

    def row_step(carry, items):
        return (carry, one_row(weights, items[0], items[1], items[2], items[3]))
    _, (layer_vals, pooled) = lax.scan(jax.checkpoint(row_step), jnp.zeros((), jnp.float32), (token_values, keep_mask, segments, cls_pos))
    first = pooled[:, :, 0].reshape(NS, D)
    second = pooled[:, :, 1].reshape(NS, D)
    pair_dots = low_back(matmul_high(first, second.T))
    inv_first = lax.rsqrt(lax.optimization_barrier(jnp.sum(first * first, axis=-1)) + NORM_EPS)
    inv_second = lax.rsqrt(lax.optimization_barrier(jnp.sum(second * second, axis=-1)) + NORM_EPS)
    cosine_matrix = pair_dots * inv_first[:, None] * inv_second[None, :]
    similarity_logits = cosine_matrix / SOFTMAX_TEMP
    loss_value = jnp.mean(jax.nn.logsumexp(similarity_logits, axis=-1) - jnp.diagonal(similarity_logits))
    return ((loss_value, layer_vals), (first, cosine_matrix, inv_first))

def reference(tokens, segments, cls_pos, keep_mask, cotangent, contrast_loss_scale, q_weight, q_bias, k_weight, v_weight, v_bias, o_weight, o_bias, norm1_gain, norm1_shift, up_weight, up_bias, down_weight, down_bias, norm2_gain, norm2_shift, pooler_weight, pool_bias):
    weights = tuple((weight_in.astype(jnp.float32) for weight_in in (q_weight, q_bias, k_weight, v_weight, v_bias, o_weight, o_bias, norm1_gain, norm1_shift, up_weight, up_bias, down_weight, down_bias, norm2_gain, norm2_shift, pooler_weight, pool_bias)))
    token_values = tokens.astype(jnp.float32)

    def objective(weight_set, token_set):
        return forward(weight_set, token_set, keep_mask, segments, cls_pos)
    (loss_value, layer_vals), pullback, (first, cosine_matrix, inv_first) = jax.vjp(objective, weights, token_values, has_aux=True)
    weight_grads, token_grad = pullback((contrast_loss_scale.astype(jnp.float32), cotangent.astype(jnp.float32)))
    alignment = jnp.mean(2.0 - 2.0 * jnp.diagonal(cosine_matrix))
    self_cos = matmul_high(first, first.T) * inv_first[:, None] * inv_first[None, :]
    uniformity = jnp.log(jnp.mean(jnp.exp(4.0 * self_cos - 4.0)))
    return (loss_value, layer_vals.astype(jnp.bfloat16), token_grad, weight_grads[0], weight_grads[1], weight_grads[2], weight_grads[3], weight_grads[4], weight_grads[5], weight_grads[6], weight_grads[7], weight_grads[8], weight_grads[9], weight_grads[10], weight_grads[11], weight_grads[12], weight_grads[13], weight_grads[14], weight_grads[15], weight_grads[16], alignment, uniformity)
```

```python
import functools

import jax
import jax.numpy as jnp
from jax import lax
from jax.experimental import pallas as pl
from jax.experimental.pallas import tpu as pltpu
from jax.sharding import PartitionSpec as P

HEAD_DIM = 64
NORM_EPS = 1e-06
SOFTMAX_TEMP = 0.05
KEEP_SCALE = 10.0 / 9.0
INV_ROOT_TWO = 0.7071067811865476
INV_ROOT_TWO_PI = 0.3989422804014327
BF = jnp.bfloat16
F32 = jnp.float32


def dot(a, b, dims=((1,), (0,)), out=F32):
    return lax.dot_general(a, b, (dims, ((), ())), preferred_element_type=F32).astype(out)


def norm_forward(values, gain, shift):
    centre = values - jnp.mean(values, axis=-1, keepdims=True)
    spread = jnp.mean(centre * centre, axis=-1, keepdims=True)
    inv_std = lax.rsqrt(spread + NORM_EPS)
    normed = centre * inv_std
    return normed * gain + shift, normed, inv_std


def norm_backward(out_grad, normed, inv_std, gain):
    hat = out_grad * gain
    in_grad = inv_std * (
        hat
        - jnp.mean(hat, axis=-1, keepdims=True)
        - normed * jnp.mean(hat * normed, axis=-1, keepdims=True)
    )
    lead = tuple(range(out_grad.ndim - 1))
    return in_grad, jnp.sum(out_grad * normed, axis=lead), jnp.sum(out_grad, axis=lead)


TILE = 128
WIN = 256


def windows(length):
    return [(a, min(max(a - 64, 0), length - WIN)) for a in range(0, length, TILE)]


def head_masks():
    lane = lax.broadcasted_iota(jnp.int32, (1, 2 * HEAD_DIM), 1)
    return (lane < HEAD_DIM).astype(BF), (lane >= HEAD_DIM).astype(BF)


def attend_kernel(length, q_ref, k_ref, v_ref, sc_ref, sw_ref, o_ref):
    m0, m1 = head_masks()
    scale = HEAD_DIM ** (-0.5)
    for t, (a, w) in enumerate(windows(length)):
        same = sc_ref[a : a + TILE, :] == sw_ref[t : t + 1, :]
        q = q_ref[a : a + TILE, :]
        k = k_ref[w : w + WIN, :]
        v = v_ref[w : w + WIN, :]
        out = None
        for mask in (m0, m1):
            s = dot(q * mask, k, ((1,), (1,))) * scale
            s = jnp.where(same, s, -1e30)
            e = jnp.exp(s - jnp.max(s, axis=-1, keepdims=True))
            p = (e / jnp.sum(e, axis=-1, keepdims=True)).astype(BF)
            part = dot(p, v * mask)
            out = part if out is None else out + part
        o_ref[a : a + TILE, :] = out.astype(BF)


def attend(q, k, v, seg_col, seg_win):
    length, width = q.shape
    block = pl.BlockSpec((length, 128), lambda i: (0, i))
    return pl.pallas_call(
        functools.partial(attend_kernel, length),
        grid=(width // 128,),
        in_specs=[
            block,
            block,
            block,
            pl.BlockSpec(seg_col.shape, lambda i: (0, 0)),
            pl.BlockSpec(seg_win.shape, lambda i: (0, 0)),
        ],
        out_specs=block,
        out_shape=jax.ShapeDtypeStruct((length, width), BF),
        cost_estimate=pl.CostEstimate(
            flops=4 * length * WIN * width, bytes_accessed=8 * length * width, transcendentals=0
        ),
        name="attend",
    )(q, k, v, seg_col, seg_win)


def attend_back_kernel(
    length, q_ref, k_ref, v_ref, g_ref, sc_ref, sw_ref, dq_ref, dk_ref, dv_ref, qb_ref, vb_ref, ka, va
):
    m0, m1 = head_masks()
    scale = HEAD_DIM ** (-0.5)
    ka[...] = jnp.zeros_like(ka)
    va[...] = jnp.zeros_like(va)
    q_sum = jnp.zeros((1, 128), F32)
    for t, (a, w) in enumerate(windows(length)):
        same = sc_ref[a : a + TILE, :] == sw_ref[t : t + 1, :]
        q = q_ref[a : a + TILE, :]
        g = g_ref[a : a + TILE, :]
        k = k_ref[w : w + WIN, :]
        v = v_ref[w : w + WIN, :]
        dq = None
        dks = None
        dvs = None
        for mask in (m0, m1):
            qm = q * mask
            gm = g * mask
            s = dot(qm, k, ((1,), (1,))) * scale
            s = jnp.where(same, s, -1e30)
            e = jnp.exp(s - jnp.max(s, axis=-1, keepdims=True))
            p = e / jnp.sum(e, axis=-1, keepdims=True)
            dp = dot(gm, v, ((1,), (1,)))
            inner = jnp.sum(p * dp, axis=-1, keepdims=True)
            ds = (p * (dp - inner)).astype(BF)
            pb = p.astype(BF)
            dq_h = dot(ds, k * mask)
            dk_h = dot(ds, qm, ((0,), (0,)))
            dv_h = dot(pb, gm, ((0,), (0,)))
            dq = dq_h if dq is None else dq + dq_h
            dks = dk_h if dks is None else dks + dk_h
            dvs = dv_h if dvs is None else dvs + dv_h
        dq = (dq * scale).astype(BF)
        dq_ref[a : a + TILE, :] = dq
        q_sum = q_sum + jnp.sum(dq.astype(F32), axis=0, keepdims=True)
        ka[w : w + WIN, :] += dks
        va[w : w + WIN, :] += dvs
    dk_ref[...] = (ka[...] * scale).astype(BF)
    dv = va[...].astype(BF)
    dv_ref[...] = dv
    qb_ref[...] = q_sum
    vb_ref[...] = jnp.sum(dv.astype(F32), axis=0, keepdims=True)


def attend_back(q, k, v, g, seg_col, seg_win):
    length, width = q.shape
    block = pl.BlockSpec((length, 128), lambda i: (0, i))
    bias = pl.BlockSpec((1, 128), lambda i: (0, i))
    wide = jax.ShapeDtypeStruct((length, width), BF)
    thin = jax.ShapeDtypeStruct((1, width), F32)
    return pl.pallas_call(
        functools.partial(attend_back_kernel, length),
        grid=(width // 128,),
        in_specs=[
            block,
            block,
            block,
            block,
            pl.BlockSpec(seg_col.shape, lambda i: (0, 0)),
            pl.BlockSpec(seg_win.shape, lambda i: (0, 0)),
        ],
        out_specs=[block, block, block, bias, bias],
        out_shape=[wide, wide, wide, thin, thin],
        scratch_shapes=[pltpu.VMEM((length, 128), F32), pltpu.VMEM((length, 128), F32)],
        cost_estimate=pl.CostEstimate(
            flops=10 * length * WIN * width, bytes_accessed=14 * length * width, transcendentals=0
        ),
        name="attend_back",
    )(q, k, v, g, seg_col, seg_win)


def swap(x, axis, bit, size):
    return lax.ppermute(x, axis, [(i, i ^ bit) for i in range(size)])


def half_of(x, axis, which):
    return lax.dynamic_index_in_dim(x, which, axis, keepdims=False)


def scatter_rows(mine, order, dp_size):
    bits = dp_size.bit_length() - 1
    rows, cols = mine.shape
    index = lax.axis_index("dp")
    left = list(range(bits))
    left = left[::-1]
    x = mine.reshape((2,) * bits + (rows // dp_size, cols))
    for bit in order:
        at = left.index(bit)
        own = (index >> bit) & 1
        sent = half_of(x, at, 1 - own).astype(BF)
        kept = half_of(x, at, own)
        got = swap(sent, "dp", 1 << bit, dp_size)
        x = kept.astype(F32) + got.astype(F32)
        left.pop(at)
        if left:
            x = x.astype(BF)
    return x


def on_device(
    dp_size,
    tokens,
    segments,
    cls_pos,
    keep_mask,
    cotangent,
    contrast_loss_scale,
    q_weight,
    q_bias,
    k_weight,
    v_weight,
    v_bias,
    o_weight,
    o_bias,
    norm1_gain,
    norm1_shift,
    up_weight,
    up_bias,
    down_weight,
    down_bias,
    norm2_gain,
    norm2_shift,
    pooler_weight,
    pool_bias,
):
    row_count, length, width = tokens.shape
    assert row_count == 1
    mp_index = lax.axis_index("mp")
    bits = dp_size.bit_length() - 1
    part = q_weight.shape[1]
    hidden = up_weight.shape[1]

    def partner(x):
        return lax.ppermute(x, "mp", [(0, 1), (1, 0)])

    biases = partner(jnp.concatenate([q_bias, v_bias, up_bias]))
    wq = (q_weight, partner(q_weight))
    wk = (k_weight, partner(k_weight))
    wv = (v_weight, partner(v_weight))
    wo = (o_weight, partner(o_weight))
    wu = (up_weight, partner(up_weight))
    wd = (down_weight, partner(down_weight))
    bq = (q_bias, biases[:part])
    bv = (v_bias, biases[part : 2 * part])
    bu = (up_bias, biases[2 * part :])

    tok = tokens[0]
    seg = lax.dynamic_slice(segments[0], (mp_index * length,), (length,))
    seg_col = seg[:, None]
    seg_win = jnp.stack([seg[w : w + WIN] for _, w in windows(length)])
    keep = keep_mask[0].transpose(1, 2, 0, 3).astype(BF)
    cot = cotangent[0].transpose(1, 0, 2)

    qs, ks, vs, mixed = [], [], [], []
    for h in range(2):
        qs.append((dot(tok, wq[h]) + bq[h]).astype(BF))
        ks.append(dot(tok, wk[h], out=BF))
        vs.append((dot(tok, wv[h]) + bv[h]).astype(BF))
        mixed.append(attend(qs[h], ks[h], vs[h], seg_col, seg_win))
    attn = dot(mixed[0], wo[0]) + dot(mixed[1], wo[1]) + o_bias
    tok32 = tok.astype(F32)
    pre1 = tok32[None] + keep[0].astype(F32) * KEEP_SCALE * attn[None]
    hid, hat1, inv1 = norm_forward(pre1, norm1_gain, norm1_shift)
    hid_low = hid.astype(BF).reshape(2 * length, width)
    gs, slopes = [], []
    for h in range(2):
        u = dot(hid_low, wu[h]) + bu[h]
        phi = 0.5 * (1.0 + lax.erf(u * INV_ROOT_TWO))
        gs.append((u * phi).astype(BF))
        slopes.append((phi + u * jnp.exp(-0.5 * u * u) * INV_ROOT_TWO_PI).astype(BF))
    down = dot(gs[0], wd[0]) + dot(gs[1], wd[1]) + down_bias
    pre2 = hid + keep[1].astype(F32) * KEEP_SCALE * down.reshape(2, length, width)
    out, hat2, inv2 = norm_forward(pre2, norm2_gain, norm2_shift)
    out_low = out.astype(BF)

    local_pos = cls_pos[0] - mp_index * length
    sent = local_pos.shape[0]
    picker = (local_pos[:, None] == jnp.arange(length, dtype=jnp.int32)[None, :]).astype(BF)
    pooled_in = jnp.concatenate([dot(picker, out_low[v], out=BF) for v in range(2)], axis=0)
    pooled = jnp.tanh(dot(pooled_in, pooler_weight) + pool_bias)
    z_mine = pooled.astype(BF)
    z = z_mine[None]
    for bit in reversed(range(bits)):
        z = jnp.concatenate([z, swap(z, "dp", 1 << bit, dp_size)], axis=0)
    z = jnp.concatenate([z, partner(z)], axis=0)
    first = z[:, :sent].reshape(-1, width)
    second = z[:, sent:].reshape(-1, width)
    total = first.shape[0]
    first_own, second_own = first[:sent], second[:sent]
    ones = jnp.ones((1, width), F32)
    r0 = lax.rsqrt(jnp.sum(jnp.square(first.astype(F32)), axis=-1) + NORM_EPS)
    r1 = lax.rsqrt(jnp.sum(jnp.square(second.astype(F32)), axis=-1) + NORM_EPS)
    del ones
    top = 1.0 / SOFTMAX_TEMP

    def col_sums(block):
        rows = dot(second, block[0], ((1,), (1,)))
        logit = rows * r1[:, None] * block[1][None, :] / SOFTMAX_TEMP
        return jnp.sum(jnp.exp(logit - top), axis=0)

    step = 512
    if total <= step:
        sums = col_sums((first, r0))
    else:
        sums = lax.map(
            col_sums, (first.reshape(-1, step, width), r0.reshape(-1, step))
        ).reshape(total)
    lse = jnp.log(sums) + top
    eye = (
        lax.broadcasted_iota(jnp.int32, (sent, total), 0)
        == lax.broadcasted_iota(jnp.int32, (sent, total), 1)
    ).astype(F32)
    factor = contrast_loss_scale / total / SOFTMAX_TEMP
    row_dots = dot(first_own, second, ((1,), (1,)))
    row_cos = row_dots * r0[:sent, None] * r1[None, :]
    row_logit = row_cos / SOFTMAX_TEMP
    lse_own = lse[:sent]
    loss_part = jnp.sum(lse_own - jnp.sum(eye * row_logit, axis=-1)) / total
    align_part = jnp.sum(2.0 - 2.0 * jnp.sum(eye * row_cos, axis=-1)) / total
    self_cos = dot(first_own, first, ((1,), (1,))) * r0[:sent, None] * r0[None, :]
    unif_part = jnp.sum(jnp.exp(4.0 * self_cos - 4.0)) / (total * total)
    row_cg = factor * (jnp.exp(row_logit - lse_own[:, None]) - eye)
    row_dd = (row_cg * r0[:sent, None] * r1[None, :]).astype(BF)
    e0 = jnp.sum(row_cg * row_dots * r1[None, :], axis=-1)
    first_grad = dot(row_dd, second) - (e0 * r0[:sent] ** 3)[:, None] * first_own.astype(F32)
    col_dots = dot(second_own, first, ((1,), (1,)))
    col_logit = col_dots * r1[:sent, None] * r0[None, :] / SOFTMAX_TEMP
    col_cg = factor * (jnp.exp(col_logit - lse[None, :]) - eye)
    col_dd = (col_cg * r1[:sent, None] * r0[None, :]).astype(BF)
    e1 = jnp.sum(col_cg * col_dots * r0[None, :], axis=-1)
    second_grad = dot(col_dd, first) - (e1 * r1[:sent] ** 3)[:, None] * second_own.astype(F32)
    pre_grad32 = jnp.concatenate([first_grad, second_grad], axis=0) * (1.0 - pooled * pooled)
    pre_grad = pre_grad32.astype(BF)
    pool_bias_grad = jnp.sum(pre_grad.astype(F32), axis=0)
    cls_grad = dot(pre_grad, pooler_weight, ((1,), (1,)))
    picker32 = picker.astype(F32)
    row_grad = jnp.stack(
        [
            lax.dot_general(
                picker32,
                cls_grad[v * sent : (v + 1) * sent],
                (((0,), (0,)), ((), ())),
                precision=lax.Precision.HIGHEST,
                preferred_element_type=F32,
            )
            for v in range(2)
        ]
    )

    dy = cot.astype(F32) + row_grad
    dr2, gain2_grad, shift2_grad = norm_backward(dy, hat2, inv2, norm2_gain)
    df = dr2 * (keep[1].astype(F32) * KEEP_SCALE)
    down_bias_grad = jnp.sum(df, axis=(0, 1))
    df_low = df.astype(BF).reshape(2 * length, width)

    def reduce_grad(halves, order):
        got = partner(halves[1])
        return scatter_rows((halves[0].astype(F32) + got.astype(F32)).astype(BF), order, dp_size)

    rest = tuple(range(2, bits))
    xy = (0, 1) + rest
    yx = (1, 0) + rest
    g_down = reduce_grad([dot(df_low, gs[h], ((0,), (0,)), BF) for h in range(2)], xy)
    dus = []
    up_bias_grads = []
    for h in range(2):
        du = (dot(df_low, wd[h], ((1,), (1,))) * slopes[h].astype(F32)).astype(BF)
        dus.append(du)
        up_bias_grads.append(jnp.sum(du.astype(F32), axis=0))
    g_up = reduce_grad([dot(hid_low, dus[h], ((0,), (0,)), BF) for h in range(2)], yx)
    pool_rows = dot(pre_grad, pooled_in, ((0,), (0,)), BF)
    pool_own = lax.dynamic_slice(pool_rows, (0, mp_index * part), (width, part))
    pool_oth = lax.dynamic_slice(pool_rows, (0, (1 - mp_index) * part), (width, part))
    g_pool = reduce_grad([pool_own, pool_oth], xy)
    dh = dot(dus[0], wu[0], ((1,), (1,))) + dot(dus[1], wu[1], ((1,), (1,)))
    dh = dr2 + dh.reshape(2, length, width)
    dr1, gain1_grad, shift1_grad = norm_backward(dh, hat1, inv1, norm1_gain)
    resid = dr1[0] + dr1[1]
    da = (dr1[0] * keep[0, 0].astype(F32) + dr1[1] * keep[0, 1].astype(F32)) * KEEP_SCALE
    o_bias_grad = jnp.sum(da, axis=0)
    da_low = da.astype(BF)
    g_o = reduce_grad([dot(da_low, mixed[h], ((0,), (0,)), BF) for h in range(2)], yx)
    dq, dk, dv, qb, vb = [], [], [], [], []
    tok_grad = resid
    for h in range(2):
        dmix = dot(da_low, wo[h], ((1,), (1,)), BF)
        a, b, c, d, e = attend_back(qs[h], ks[h], vs[h], dmix, seg_col, seg_win)
        dq.append(a)
        dk.append(b)
        dv.append(c)
        qb.append(d[0])
        vb.append(e[0])
    g_q = reduce_grad([dot(tok, dq[h], ((0,), (0,)), BF) for h in range(2)], xy)
    g_k = reduce_grad([dot(tok, dk[h], ((0,), (0,)), BF) for h in range(2)], yx)
    g_v = reduce_grad([dot(tok, dv[h], ((0,), (0,)), BF) for h in range(2)], xy)
    for h in range(2):
        tok_grad = tok_grad + dot(dq[h], wq[h], ((1,), (1,)))
        tok_grad = tok_grad + dot(dk[h], wk[h], ((1,), (1,)))
        tok_grad = tok_grad + dot(dv[h], wv[h], ((1,), (1,)))

    def in_place(pair):
        low = jnp.where(mp_index == 0, pair[0], pair[1])
        high = jnp.where(mp_index == 0, pair[1], pair[0])
        return jnp.concatenate([low, high])

    pieces = [
        gain1_grad,
        shift1_grad,
        o_bias_grad,
        gain2_grad,
        shift2_grad,
        down_bias_grad,
        pool_bias_grad,
        in_place(qb),
        in_place(vb),
        in_place(up_bias_grads),
        jnp.pad(jnp.stack([loss_part, align_part, unif_part]), (0, 125)),
    ]
    small = jnp.concatenate(pieces)
    small = small + partner(small)
    for bit in range(bits):
        small = small + swap(small, "dp", 1 << bit, dp_size)
    outs = []
    at = 0
    for piece in pieces:
        outs.append(small[at : at + piece.shape[0]])
        at += piece.shape[0]
    scalars = outs[10]
    return (
        scalars[0],
        out_low.transpose(1, 0, 2)[None],
        tok_grad[None],
        g_q,
        outs[7],
        g_k,
        g_v,
        outs[8],
        g_o.T,
        outs[2],
        outs[0],
        outs[1],
        g_up,
        outs[9],
        g_down.T,
        outs[5],
        outs[3],
        outs[4],
        g_pool.T,
        outs[6],
        scalars[1],
        jnp.log(scalars[2]),
    )


def solution(mesh):
    rep = P()
    in_specs = (
        P("dp", "mp", None),
        P("dp", None),
        P("dp", "mp"),
        P("dp", "mp", None, None, None),
        P("dp", "mp", None, None),
        rep,
        P(None, "mp"),
        P("mp"),
        P(None, "mp"),
        P(None, "mp"),
        P("mp"),
        P("mp", None),
        rep,
        rep,
        rep,
        P(None, "mp"),
        P("mp"),
        P("mp", None),
        rep,
        rep,
        rep,
        rep,
        rep,
    )
    out_specs = (
        rep,
        P("dp", "mp", None, None),
        P("dp", "mp", None),
        P("dp", "mp"),
        rep,
        P("dp", "mp"),
        P("dp", "mp"),
        rep,
        P("mp", "dp"),
        rep,
        rep,
        rep,
        P("dp", "mp"),
        rep,
        P("mp", "dp"),
        rep,
        rep,
        rep,
        P("mp", "dp"),
        rep,
        rep,
        rep,
    )
    return jax.shard_map(
        functools.partial(on_device, mesh.shape["dp"]),
        mesh=mesh,
        in_specs=in_specs,
        out_specs=out_specs,
        check_vma=False,
    )
```

```python
import functools

import jax
import jax.numpy as jnp
from jax import lax
from jax.experimental import pallas as pl
from jax.experimental.pallas import tpu as pltpu
from jax.sharding import PartitionSpec as P


HEAD_DIM = 64
NORM_EPS = 1e-06
SOFTMAX_TEMP = 0.05
KEEP_SCALE = 10.0 / 9.0
INV_ROOT_TWO = 0.7071067811865476
INV_ROOT_TWO_PI = 0.3989422804014327
BF = jnp.bfloat16
F32 = jnp.float32


def dot(a, b, dims=((1,), (0,)), out=F32):
    return lax.dot_general(a, b, (dims, ((), ())), preferred_element_type=F32).astype(out)


def norm_forward(values, gain, shift):
    centre = values - jnp.mean(values, axis=-1, keepdims=True)
    spread = jnp.mean(centre * centre, axis=-1, keepdims=True)
    inv_std = lax.rsqrt(spread + NORM_EPS)
    normed = centre * inv_std
    return normed * gain + shift, normed, inv_std


def norm_backward(out_grad, normed, inv_std, gain):
    hat = out_grad * gain
    in_grad = inv_std * (
        hat
        - jnp.mean(hat, axis=-1, keepdims=True)
        - normed * jnp.mean(hat * normed, axis=-1, keepdims=True)
    )
    lead = tuple(range(out_grad.ndim - 1))
    return in_grad, jnp.sum(out_grad * normed, axis=lead), jnp.sum(out_grad, axis=lead)


TILE = 128
WIN = 256


def windows(length):
    return [(a, min(max(a - 64, 0), length - WIN)) for a in range(0, length, TILE)]


def head_masks():
    lane = lax.broadcasted_iota(jnp.int32, (1, 2 * HEAD_DIM), 1)
    return (lane < HEAD_DIM).astype(BF), (lane >= HEAD_DIM).astype(BF)


def attend_kernel(length, q_ref, k_ref, v_ref, sc_ref, sw_ref, o_ref):
    m0, m1 = head_masks()
    scale = HEAD_DIM ** (-0.5)
    for t, (a, w) in enumerate(windows(length)):
        same = sc_ref[a : a + TILE, :] == sw_ref[t : t + 1, :]
        q = q_ref[a : a + TILE, :]
        k = k_ref[w : w + WIN, :]
        v = v_ref[w : w + WIN, :]
        out = None
        for mask in (m0, m1):
            s = dot(q * mask, k, ((1,), (1,))) * scale
            s = jnp.where(same, s, -1e30)
            e = jnp.exp(s - jnp.max(s, axis=-1, keepdims=True))
            p = (e / jnp.sum(e, axis=-1, keepdims=True)).astype(BF)
            part = dot(p, v * mask)
            out = part if out is None else out + part
        o_ref[a : a + TILE, :] = out.astype(BF)


def attend(q, k, v, seg_col, seg_win):
    length, width = q.shape
    block = pl.BlockSpec((length, 128), lambda i: (0, i))
    return pl.pallas_call(
        functools.partial(attend_kernel, length),
        grid=(width // 128,),
        in_specs=[
            block,
            block,
            block,
            pl.BlockSpec(seg_col.shape, lambda i: (0, 0)),
            pl.BlockSpec(seg_win.shape, lambda i: (0, 0)),
        ],
        out_specs=block,
        out_shape=jax.ShapeDtypeStruct((length, width), BF),
        cost_estimate=pl.CostEstimate(
            flops=4 * length * WIN * width, bytes_accessed=8 * length * width, transcendentals=0
        ),
        name="attend",
    )(q, k, v, seg_col, seg_win)


def attend_back_kernel(length, q_ref, k_ref, v_ref, g_ref, sc_ref, sw_ref, d_ref, b_ref, ka, va):
    pair = pl.program_id(0)
    pairs = pl.num_programs(0)

    def lanes(which):
        return pl.ds(pl.multiple_of((which * pairs + pair) * 128, 128), 128)

    m0, m1 = head_masks()
    scale = HEAD_DIM ** (-0.5)
    ka[...] = jnp.zeros_like(ka)
    va[...] = jnp.zeros_like(va)
    q_sum = jnp.zeros((1, 128), F32)
    for t, (a, w) in enumerate(windows(length)):
        same = sc_ref[a : a + TILE, :] == sw_ref[t : t + 1, :]
        q = q_ref[a : a + TILE, :]
        g = g_ref[a : a + TILE, :]
        k = k_ref[w : w + WIN, :]
        v = v_ref[w : w + WIN, :]
        dq = None
        dks = None
        dvs = None
        for mask in (m0, m1):
            qm = q * mask
            gm = g * mask
            s = dot(qm, k, ((1,), (1,))) * scale
            s = jnp.where(same, s, -1e30)
            e = jnp.exp(s - jnp.max(s, axis=-1, keepdims=True))
            p = e / jnp.sum(e, axis=-1, keepdims=True)
            dp = dot(gm, v, ((1,), (1,)))
            inner = jnp.sum(p * dp, axis=-1, keepdims=True)
            ds = (p * (dp - inner)).astype(BF)
            pb = p.astype(BF)
            dq_h = dot(ds, k * mask)
            dk_h = dot(ds, qm, ((0,), (0,)))
            dv_h = dot(pb, gm, ((0,), (0,)))
            dq = dq_h if dq is None else dq + dq_h
            dks = dk_h if dks is None else dks + dk_h
            dvs = dv_h if dvs is None else dvs + dv_h
        dq = (dq * scale).astype(BF)
        d_ref[a : a + TILE, lanes(0)] = dq
        q_sum = q_sum + jnp.sum(dq.astype(F32), axis=0, keepdims=True)
        ka[w : w + WIN, :] += dks
        va[w : w + WIN, :] += dvs
    d_ref[:, lanes(1)] = (ka[...] * scale).astype(BF)
    dv = va[...].astype(BF)
    d_ref[:, lanes(2)] = dv
    b_ref[:, lanes(0)] = q_sum
    b_ref[:, lanes(1)] = jnp.sum(dv.astype(F32), axis=0, keepdims=True)


def attend_back(q, k, v, g, seg_col, seg_win):
    length, width = q.shape
    block = pl.BlockSpec((length, 128), lambda i: (0, i))
    return pl.pallas_call(
        functools.partial(attend_back_kernel, length),
        grid=(width // 128,),
        in_specs=[
            block,
            block,
            block,
            block,
            pl.BlockSpec(seg_col.shape, lambda i: (0, 0)),
            pl.BlockSpec(seg_win.shape, lambda i: (0, 0)),
        ],
        out_specs=[
            pl.BlockSpec((length, 3 * width), lambda i: (0, 0)),
            pl.BlockSpec((1, 2 * width), lambda i: (0, 0)),
        ],
        out_shape=[
            jax.ShapeDtypeStruct((length, 3 * width), BF),
            jax.ShapeDtypeStruct((1, 2 * width), F32),
        ],
        scratch_shapes=[pltpu.VMEM((length, 128), F32), pltpu.VMEM((length, 128), F32)],
        cost_estimate=pl.CostEstimate(
            flops=10 * length * WIN * width, bytes_accessed=14 * length * width, transcendentals=0
        ),
        name="attend_back",
    )(q, k, v, g, seg_col, seg_win)


def contrast_kernel(
    own, block, z_ref, pooled_ref, pw_ref, scale_ref, pg_ref, pb_ref, hl_ref, sc_ref, f_ref, s_ref, r0_ref, r1_ref, sum_ref
):
    total, width = f_ref.shape
    top = 1.0 / SOFTMAX_TEMP

    def split(i, carry):
        to = pl.ds(pl.multiple_of(i * own, own), own)
        f_ref[to, :] = z_ref[pl.ds(pl.multiple_of(2 * i * own, own), own), :]
        s_ref[to, :] = z_ref[pl.ds(pl.multiple_of((2 * i + 1) * own, own), own), :]
        return carry

    lax.fori_loop(0, total // own, split, 0)

    def inverse(values):
        values = values.astype(F32)
        return lax.rsqrt(jnp.sum(values * values, axis=-1, keepdims=True) + NORM_EPS)

    def lay(column):
        return jnp.transpose(jnp.broadcast_to(column, (block, 128)))[0:1, :]

    def norms(i, carry):
        at = pl.ds(pl.multiple_of(i * block, block), block)
        r0_ref[:, at] = lay(inverse(f_ref[at, :]))
        r1_ref[:, at] = lay(inverse(s_ref[at, :]))
        return carry

    lax.fori_loop(0, total // block, norms, 0)
    r0 = r0_ref[...]
    r1 = r1_ref[...]
    sum_ref[...] = jnp.zeros_like(sum_ref)

    def column_sums(i, carry):
        at = pl.ds(pl.multiple_of(i * block, block), block)
        rows = s_ref[at, :]
        logit = dot(rows, f_ref[...], ((1,), (1,))) * (inverse(rows) * top) * r0
        sum_ref[...] += jnp.sum(jnp.exp(logit - top), axis=0, keepdims=True)
        return carry

    lax.fori_loop(0, total // block, column_sums, 0)
    lse_row = jnp.log(sum_ref[...]) + top
    first = f_ref[...]
    second = s_ref[...]
    first_own = f_ref[0:own, :]
    second_own = s_ref[0:own, :]
    r0_own = inverse(first_own)
    r1_own = inverse(second_own)
    eye = (
        lax.broadcasted_iota(jnp.int32, (own, total), 0)
        == lax.broadcasted_iota(jnp.int32, (own, total), 1)
    ).astype(F32)
    factor = scale_ref[0, 0] * (top / total)
    row_dots = dot(first_own, second, ((1,), (1,)))
    row_cos = row_dots * r0_own * r1
    row_logit = row_cos * top
    lse_own = jnp.log(jnp.sum(jnp.exp(row_logit - top), axis=-1, keepdims=True)) + top
    loss = (
        jnp.sum(lse_own - jnp.sum(eye * row_logit, axis=-1, keepdims=True), axis=0, keepdims=True)
        / total
    )
    align = (
        jnp.sum(
            2.0 - 2.0 * jnp.sum(eye * row_cos, axis=-1, keepdims=True), axis=0, keepdims=True
        )
        / total
    )
    self_cos = dot(first_own, first, ((1,), (1,))) * r0_own * r0
    unif = jnp.sum(
        jnp.sum(jnp.exp(4.0 * self_cos - 4.0), axis=-1, keepdims=True), axis=0, keepdims=True
    ) / (total * total)
    row_cg = factor * (jnp.exp(row_logit - lse_own) - eye)
    row_dd = (row_cg * r0_own * r1).astype(BF)
    e0 = jnp.sum(row_cg * row_dots * r1, axis=-1, keepdims=True)
    grad0 = dot(row_dd, second) - (e0 * r0_own * r0_own * r0_own) * first_own.astype(F32)
    col_dots = dot(second_own, first, ((1,), (1,)))
    col_cg = factor * (jnp.exp(col_dots * r1_own * r0 * top - lse_row) - eye)
    col_dd = (col_cg * r1_own * r0).astype(BF)
    e1 = jnp.sum(col_cg * col_dots * r0, axis=-1, keepdims=True)
    grad1 = dot(col_dd, first) - (e1 * r1_own * r1_own * r1_own) * second_own.astype(F32)
    bias = jnp.zeros((1, width), F32)
    for v, grad in enumerate((grad0, grad1)):
        pooled = pooled_ref[v * own : (v + 1) * own, :]
        pre = (grad * (1.0 - pooled * pooled)).astype(BF)
        pg_ref[v * own : (v + 1) * own, :] = pre
        bias = bias + jnp.sum(pre.astype(F32), axis=0, keepdims=True)
        back = dot(pre, pw_ref[...], ((1,), (1,)))
        high = back.astype(BF)
        hl_ref[2 * v * own : (2 * v + 1) * own, :] = high
        hl_ref[(2 * v + 1) * own : (2 * v + 2) * own, :] = (back - high.astype(F32)).astype(BF)
    pb_ref[...] = bias
    lane = lax.broadcasted_iota(jnp.int32, (1, 128), 1)
    sc_ref[...] = jnp.where(
        lane == 0, loss, jnp.where(lane == 1, align, jnp.where(lane == 2, unif, 0.0))
    )


def contrast(z, pooled, pooler_weight, loss_scale):
    own = pooled.shape[0] // 2
    total = z.shape[0] // 2
    width = z.shape[1]
    block = min(512, total)
    vmem = pl.BlockSpec(memory_space=pltpu.VMEM)
    return pl.pallas_call(
        functools.partial(contrast_kernel, own, block),
        in_specs=[vmem, vmem, vmem, pl.BlockSpec(memory_space=pltpu.SMEM)],
        out_specs=[vmem] * 4,
        out_shape=[
            jax.ShapeDtypeStruct((2 * own, width), BF),
            jax.ShapeDtypeStruct((1, width), F32),
            jax.ShapeDtypeStruct((4 * own, width), BF),
            jax.ShapeDtypeStruct((1, 128), F32),
        ],
        scratch_shapes=[
            pltpu.VMEM((total, width), BF),
            pltpu.VMEM((total, width), BF),
            pltpu.VMEM((1, total), F32),
            pltpu.VMEM((1, total), F32),
            pltpu.VMEM((1, total), F32),
        ],
        cost_estimate=pl.CostEstimate(
            flops=2 * total * total * width, bytes_accessed=8 * total * width, transcendentals=0
        ),
        name="contrast",
    )(z, pooled, pooler_weight, loss_scale.reshape(1, 1))


def swap(x, axis, bit, size):
    return lax.ppermute(x, axis, [(i, i ^ bit) for i in range(size)])


def half_of(x, axis, which):
    return lax.dynamic_index_in_dim(x, which, axis, keepdims=False)


def scatter_rows(mine, order, dp_size):
    bits = dp_size.bit_length() - 1
    rows, cols = mine.shape
    index = lax.axis_index("dp")
    left = list(range(bits))[::-1]
    x = mine.reshape((2,) * bits + (rows // dp_size, cols))
    for bit in order:
        at = left.index(bit)
        own = (index >> bit) & 1
        sent = half_of(x, at, 1 - own).astype(BF)
        kept = half_of(x, at, own)
        got = swap(sent, "dp", 1 << bit, dp_size)
        x = kept.astype(F32) + got.astype(F32)
        left.pop(at)
        if left:
            x = x.astype(BF)
    return x


def on_device(
    dp_size,
    tokens,
    segments,
    cls_pos,
    keep_mask,
    cotangent,
    contrast_loss_scale,
    q_weight,
    q_bias,
    k_weight,
    v_weight,
    v_bias,
    o_weight,
    o_bias,
    norm1_gain,
    norm1_shift,
    up_weight,
    up_bias,
    down_weight,
    down_bias,
    norm2_gain,
    norm2_shift,
    pooler_weight,
    pool_bias,
):
    row_count, length, width = tokens.shape
    assert row_count == 1
    mp_index = lax.axis_index("mp")
    bits = dp_size.bit_length() - 1
    part = q_weight.shape[1]

    def partner(x):
        return lax.ppermute(x, "mp", [(0, 1), (1, 0)])

    biases = partner(jnp.concatenate([q_bias, v_bias, up_bias]))
    wq = (q_weight, partner(q_weight))
    wk = (k_weight, partner(k_weight))
    wv = (v_weight, partner(v_weight))
    wo = (o_weight, partner(o_weight))
    wu = (up_weight, partner(up_weight))
    wd = (down_weight, partner(down_weight))
    bq = (q_bias, biases[:part])
    bv = (v_bias, biases[part : 2 * part])
    bu = (up_bias, biases[2 * part :])

    tok = tokens[0]
    seg = lax.dynamic_slice(segments[0], (mp_index * length,), (length,))
    seg_col = seg[:, None]
    seg_win = jnp.stack([seg[w : w + WIN] for _, w in windows(length)])
    keep = keep_mask[0].transpose(1, 2, 0, 3).astype(BF)
    cot = cotangent[0].transpose(1, 0, 2)

    qs, ks, vs, mixed = [], [], [], []
    for h in range(2):
        qs.append((dot(tok, wq[h]) + bq[h]).astype(BF))
        ks.append(dot(tok, wk[h], out=BF))
        vs.append((dot(tok, wv[h]) + bv[h]).astype(BF))
        mixed.append(attend(qs[h], ks[h], vs[h], seg_col, seg_win))
    attn = dot(mixed[0], wo[0]) + dot(mixed[1], wo[1]) + o_bias
    tok32 = tok.astype(F32)
    pre1 = tok32[None] + keep[0].astype(F32) * KEEP_SCALE * attn[None]
    hid, hat1, inv1 = norm_forward(pre1, norm1_gain, norm1_shift)
    hid_low = hid.astype(BF).reshape(2 * length, width)
    gs, slopes = [], []
    for h in range(2):
        u = dot(hid_low, wu[h]) + bu[h]
        phi = 0.5 * (1.0 + lax.erf(u * INV_ROOT_TWO))
        gs.append((u * phi).astype(BF))
        slopes.append((phi + u * jnp.exp(-0.5 * u * u) * INV_ROOT_TWO_PI).astype(BF))
    down = dot(gs[0], wd[0]) + dot(gs[1], wd[1]) + down_bias
    pre2 = hid + keep[1].astype(F32) * KEEP_SCALE * down.reshape(2, length, width)
    out, hat2, inv2 = norm_forward(pre2, norm2_gain, norm2_shift)
    out_low = out.astype(BF)

    local_pos = cls_pos[0] - mp_index * length
    sent = local_pos.shape[0]
    picker = (local_pos[:, None] == jnp.arange(length, dtype=jnp.int32)[None, :]).astype(BF)
    pooled_in = jnp.concatenate([dot(picker, out_low[v], out=BF) for v in range(2)], axis=0)
    pooled = jnp.tanh(dot(pooled_in, pooler_weight) + pool_bias)
    z = pooled.astype(BF)
    for bit in reversed(range(bits)):
        other = swap(z, "dp", 1 << bit, dp_size)
        z = jnp.concatenate([z, other], axis=0)
    other = partner(z)
    z = jnp.concatenate([z, other], axis=0)
    pre_grad, pool_bias_grad, high_low, scalars = contrast(
        z, pooled, pooler_weight, contrast_loss_scale
    )
    picker2 = jnp.concatenate([picker, picker], axis=0)
    row_grad = jnp.stack(
        [dot(picker2, high_low[2 * v * sent : 2 * (v + 1) * sent], ((0,), (0,))) for v in range(2)]
    )

    dy = cot.astype(F32) + row_grad
    dr2, gain2_grad, shift2_grad = norm_backward(dy, hat2, inv2, norm2_gain)
    df = dr2 * (keep[1].astype(F32) * KEEP_SCALE)
    down_bias_grad = jnp.sum(df, axis=(0, 1))
    df_low = df.astype(BF).reshape(2 * length, width)

    def reduce_grad(left, right, order):
        sent = dot(left(1), right(1), ((0,), (0,)), BF)
        got = partner(sent)
        both = (dot(left(0), right(0), ((0,), (0,))) + got.astype(F32)).astype(BF)
        return scatter_rows(both, order, dp_size)

    rest = tuple(range(3, bits))
    xyz = (0, 1, 2) + rest
    yxz = (1, 0, 2) + rest
    zxy = (2, 0, 1) + rest
    g_down = reduce_grad(lambda h: df_low, lambda h: gs[h], xyz)
    dus = []
    up_bias_grads = []
    for h in range(2):
        du = (dot(df_low, wd[h], ((1,), (1,))) * slopes[h].astype(F32)).astype(BF)
        up_bias_grads.append(jnp.sum(du.astype(F32), axis=0))
        dus.append(du)
    g_up = reduce_grad(lambda h: hid_low, lambda h: dus[h], yxz)
    dh = dot(dus[0], wu[0], ((1,), (1,))) + dot(dus[1], wu[1], ((1,), (1,)))
    dh = dr2 + dh.reshape(2, length, width)
    dr1, gain1_grad, shift1_grad = norm_backward(dh, hat1, inv1, norm1_gain)
    resid = dr1[0] + dr1[1]
    da = (dr1[0] * keep[0, 0].astype(F32) + dr1[1] * keep[0, 1].astype(F32)) * KEEP_SCALE
    o_bias_grad = jnp.sum(da, axis=0)
    da_low = da.astype(BF)
    pool_rows = dot(pre_grad, pooled_in, ((0,), (0,)), BF)
    pool_half = [
        lax.dynamic_slice(pool_rows, (0, which * part), (width, part))
        for which in (mp_index, 1 - mp_index)
    ]
    sent = jnp.concatenate([dot(da_low, mixed[1], ((0,), (0,)), BF), pool_half[1]], axis=1)
    got = partner(sent)
    both = jnp.concatenate([dot(da_low, mixed[0], ((0,), (0,)), BF), pool_half[0]], axis=1)
    both = (both.astype(F32) + got.astype(F32)).astype(BF)
    g_c = scatter_rows(both, zxy, dp_size)
    g_o, g_pool = g_c[:, :part], g_c[:, part:]
    joint, bias_sums = [None] * 2, [None] * 2
    for h in (1, 0):
        dmix = dot(da_low, wo[h], ((1,), (1,)), BF)
        joint[h], bias_sums[h] = attend_back(qs[h], ks[h], vs[h], dmix, seg_col, seg_win)
    cut = 5 * (3 * part // 9)
    g_j1 = reduce_grad(lambda h: tok, lambda h: joint[h][:, :cut], xyz)
    g_j2 = reduce_grad(lambda h: tok, lambda h: joint[h][:, cut:], yxz)
    g_joint = jnp.concatenate([g_j1, g_j2], axis=1)
    g_q, g_k, g_v = (g_joint[:, i * part : (i + 1) * part] for i in range(3))
    qb = [b[0, :part] for b in bias_sums]
    vb = [b[0, part:] for b in bias_sums]
    tok_grad = resid
    for h in range(2):
        for i, w in enumerate((wq, wk, wv)):
            tok_grad = tok_grad + dot(joint[h][:, i * part : (i + 1) * part], w[h], ((1,), (1,)))

    def in_place(pair):
        low = jnp.where(mp_index == 0, pair[0], pair[1])
        high = jnp.where(mp_index == 0, pair[1], pair[0])
        return jnp.concatenate([low, high])

    pieces = [
        gain1_grad,
        shift1_grad,
        o_bias_grad,
        gain2_grad,
        shift2_grad,
        down_bias_grad,
        pool_bias_grad[0],
        in_place(qb),
        in_place(vb),
        in_place(up_bias_grads),
        scalars[0],
    ]
    small = jnp.concatenate(pieces)
    got = partner(small)
    small = small + got
    for bit in range(bits):
        got = swap(small, "dp", 1 << bit, dp_size)
        small = small + got
    outs = []
    at = 0
    for piece in pieces:
        outs.append(small[at : at + piece.shape[0]])
        at += piece.shape[0]
    scalars = outs[10]
    return (
        scalars[0],
        out_low.transpose(1, 0, 2)[None],
        tok_grad[None],
        g_q,
        outs[7],
        g_k,
        g_v,
        outs[8],
        g_o.T,
        outs[2],
        outs[0],
        outs[1],
        g_up,
        outs[9],
        g_down.T,
        outs[5],
        outs[3],
        outs[4],
        g_pool.T,
        outs[6],
        scalars[1],
        jnp.log(scalars[2]),
    )


def solution(mesh):
    rep = P()
    in_specs = (
        P("dp", "mp", None),
        P("dp", None),
        P("dp", "mp"),
        P("dp", "mp", None, None, None),
        P("dp", "mp", None, None),
        rep,
        P(None, "mp"),
        P("mp"),
        P(None, "mp"),
        P(None, "mp"),
        P("mp"),
        P("mp", None),
        rep,
        rep,
        rep,
        P(None, "mp"),
        P("mp"),
        P("mp", None),
        rep,
        rep,
        rep,
        rep,
        rep,
    )
    out_specs = (
        rep,
        P("dp", "mp", None, None),
        P("dp", "mp", None),
        P("dp", "mp"),
        rep,
        P("dp", "mp"),
        P("dp", "mp"),
        rep,
        P("mp", "dp"),
        rep,
        rep,
        rep,
        P("dp", "mp"),
        rep,
        P("mp", "dp"),
        rep,
        rep,
        rep,
        P("mp", "dp"),
        rep,
        rep,
        rep,
    )

    def body(*args):
        return on_device(mesh.shape["dp"], *args)

    return jax.shard_map(body, mesh=mesh, in_specs=in_specs, out_specs=out_specs, check_vma=False)
```

```python
import functools

import jax
import jax.numpy as jnp
from jax import lax
from jax.experimental import pallas as pl
from jax.experimental.pallas import tpu as pltpu
from jax.sharding import PartitionSpec as P


HEAD_DIM = 64
NORM_EPS = 1e-06
SOFTMAX_TEMP = 0.05
KEEP_SCALE = 10.0 / 9.0
INV_ROOT_TWO = 0.7071067811865476
INV_ROOT_TWO_PI = 0.3989422804014327
BF = jnp.bfloat16
F32 = jnp.float32


def dot(a, b, dims=((1,), (0,)), out=F32):
    return lax.dot_general(a, b, (dims, ((), ())), preferred_element_type=F32).astype(out)


def norm_forward(values, gain, shift):
    centre = values - jnp.mean(values, axis=-1, keepdims=True)
    spread = jnp.mean(centre * centre, axis=-1, keepdims=True)
    inv_std = lax.rsqrt(spread + NORM_EPS)
    normed = centre * inv_std
    return normed * gain + shift, normed, inv_std


def norm_backward(out_grad, normed, inv_std, gain):
    hat = out_grad * gain
    in_grad = inv_std * (
        hat
        - jnp.mean(hat, axis=-1, keepdims=True)
        - normed * jnp.mean(hat * normed, axis=-1, keepdims=True)
    )
    lead = tuple(range(out_grad.ndim - 1))
    return in_grad, jnp.sum(out_grad * normed, axis=lead), jnp.sum(out_grad, axis=lead)


TILE = 128
WIN = 256


def windows(length):
    return [(a, min(max(a - 64, 0), length - WIN)) for a in range(0, length, TILE)]


def head_masks():
    lane = lax.broadcasted_iota(jnp.int32, (1, 2 * HEAD_DIM), 1)
    return (lane < HEAD_DIM).astype(BF), (lane >= HEAD_DIM).astype(BF)


def attend_kernel(length, x_ref, wq_ref, wk_ref, wv_ref, bq_ref, bv_ref, sc_ref, sw_ref, q_ref, k_ref, v_ref, o_ref):
    pair = pl.program_id(0)

    @pl.when(pair == 0)
    def _():
        x = x_ref[...]
        q_ref[...] = (dot(x, wq_ref[...]) + bq_ref[...]).astype(BF)
        k_ref[...] = dot(x, wk_ref[...], out=BF)
        v_ref[...] = (dot(x, wv_ref[...]) + bv_ref[...]).astype(BF)

    lanes = pl.ds(pl.multiple_of(pair * 128, 128), 128)
    m0, m1 = head_masks()
    scale = HEAD_DIM ** (-0.5)
    ones = jnp.ones((WIN, 128), BF)
    for t, (a, w) in enumerate(windows(length)):
        same = sc_ref[a : a + TILE, :] == sw_ref[t : t + 1, :]
        q = q_ref[a : a + TILE, lanes]
        k = k_ref[w : w + WIN, lanes]
        v = v_ref[w : w + WIN, lanes]
        out = None
        for mask in (m0, m1):
            s = dot(q * mask, k, ((1,), (1,))) * scale
            s = jnp.where(same, s, -1e30)
            e = jnp.exp(s - jnp.max(s, axis=-1, keepdims=True)).astype(BF)
            both = dot(e, jnp.concatenate([v * mask, ones], axis=1))
            part = both[:, :128] / both[:, 128:]
            out = part if out is None else out + part
        o_ref[a : a + TILE, :] = out.astype(BF)


def attend(x, wq, wk, wv, bq, bv, seg_col, seg_win):
    length, depth = x.shape
    width = wq.shape[1]
    whole = lambda shape: pl.BlockSpec(shape, lambda i: (0, 0))
    wide = jax.ShapeDtypeStruct((length, width), BF)
    return pl.pallas_call(
        functools.partial(attend_kernel, length),
        grid=(width // 128,),
        in_specs=[
            whole((length, depth)),
            whole((depth, width)),
            whole((depth, width)),
            whole((depth, width)),
            whole((1, width)),
            whole((1, width)),
            whole(seg_col.shape),
            whole(seg_win.shape),
        ],
        out_specs=[
            whole((length, width)),
            whole((length, width)),
            whole((length, width)),
            pl.BlockSpec((length, 128), lambda i: (0, i)),
        ],
        out_shape=[wide] * 4,
        cost_estimate=pl.CostEstimate(
            flops=6 * length * depth * width + 4 * length * WIN * width,
            bytes_accessed=6 * depth * width + 10 * length * width,
            transcendentals=0,
        ),
        name="attend",
    )(x, wq, wk, wv, bq.reshape(1, -1), bv.reshape(1, -1), seg_col, seg_win)


def attend_back_kernel(length, q_ref, k_ref, v_ref, g_ref, sc_ref, sw_ref, d_ref, b_ref, ka, va):
    pair = pl.program_id(0)
    pairs = pl.num_programs(0)

    def lanes(which):
        return pl.ds(pl.multiple_of((which * pairs + pair) * 128, 128), 128)

    m0, m1 = head_masks()
    scale = HEAD_DIM ** (-0.5)
    ka[...] = jnp.zeros_like(ka)
    va[...] = jnp.zeros_like(va)
    q_sum = jnp.zeros((1, 128), F32)
    for t, (a, w) in enumerate(windows(length)):
        same = sc_ref[a : a + TILE, :] == sw_ref[t : t + 1, :]
        q = q_ref[a : a + TILE, :]
        g = g_ref[a : a + TILE, :]
        k = k_ref[w : w + WIN, :]
        v = v_ref[w : w + WIN, :]
        dq = None
        dks = None
        dvs = None
        for mask in (m0, m1):
            qm = q * mask
            gm = g * mask
            s = dot(qm, k, ((1,), (1,))) * scale
            s = jnp.where(same, s, -1e30)
            e = jnp.exp(s - jnp.max(s, axis=-1, keepdims=True))
            p = e / jnp.sum(e, axis=-1, keepdims=True)
            dp = dot(gm, v, ((1,), (1,)))
            inner = jnp.sum(p * dp, axis=-1, keepdims=True)
            ds = (p * (dp - inner)).astype(BF)
            pb = p.astype(BF)
            dq_h = dot(ds, k * mask)
            dk_h = dot(ds, qm, ((0,), (0,)))
            dv_h = dot(pb, gm, ((0,), (0,)))
            dq = dq_h if dq is None else dq + dq_h
            dks = dk_h if dks is None else dks + dk_h
            dvs = dv_h if dvs is None else dvs + dv_h
        dq = (dq * scale).astype(BF)
        d_ref[a : a + TILE, lanes(0)] = dq
        q_sum = q_sum + jnp.sum(dq.astype(F32), axis=0, keepdims=True)
        ka[w : w + WIN, :] += dks
        va[w : w + WIN, :] += dvs
    d_ref[:, lanes(1)] = (ka[...] * scale).astype(BF)
    dv = va[...].astype(BF)
    d_ref[:, lanes(2)] = dv
    b_ref[:, lanes(0)] = q_sum
    b_ref[:, lanes(1)] = jnp.sum(dv.astype(F32), axis=0, keepdims=True)


def attend_back(q, k, v, g, seg_col, seg_win):
    length, width = q.shape
    block = pl.BlockSpec((length, 128), lambda i: (0, i))
    return pl.pallas_call(
        functools.partial(attend_back_kernel, length),
        grid=(width // 128,),
        in_specs=[
            block,
            block,
            block,
            block,
            pl.BlockSpec(seg_col.shape, lambda i: (0, 0)),
            pl.BlockSpec(seg_win.shape, lambda i: (0, 0)),
        ],
        out_specs=[
            pl.BlockSpec((length, 3 * width), lambda i: (0, 0)),
            pl.BlockSpec((1, 2 * width), lambda i: (0, 0)),
        ],
        out_shape=[
            jax.ShapeDtypeStruct((length, 3 * width), BF),
            jax.ShapeDtypeStruct((1, 2 * width), F32),
        ],
        scratch_shapes=[pltpu.VMEM((length, 128), F32), pltpu.VMEM((length, 128), F32)],
        cost_estimate=pl.CostEstimate(
            flops=10 * length * WIN * width, bytes_accessed=14 * length * width, transcendentals=0
        ),
        name="attend_back",
    )(q, k, v, g, seg_col, seg_win)


def contrast_kernel(
    own, block, za_ref, zb_ref, pooled_ref, pw_ref, scale_ref, pg_ref, pb_ref, hl_ref, sc_ref, f_ref, s_ref, r0_ref, r1_ref, sum_ref
):
    total, width = f_ref.shape
    top = 1.0 / SOFTMAX_TEMP

    for half, z_ref in enumerate((za_ref, zb_ref)):

        def split(i, carry, half=half, z_ref=z_ref):
            to = pl.ds(pl.multiple_of(i * own + half * (total // 2), own), own)
            f_ref[to, :] = z_ref[pl.ds(pl.multiple_of(2 * i * own, own), own), :]
            s_ref[to, :] = z_ref[pl.ds(pl.multiple_of((2 * i + 1) * own, own), own), :]
            return carry

        lax.fori_loop(0, total // own // 2, split, 0)

    def inverse(values):
        values = values.astype(F32)
        return lax.rsqrt(jnp.sum(values * values, axis=-1, keepdims=True) + NORM_EPS)

    def lay(column):
        return jnp.transpose(jnp.broadcast_to(column, (block, 128)))[0:1, :]

    def norms(i, carry):
        at = pl.ds(pl.multiple_of(i * block, block), block)
        r0_ref[:, at] = lay(inverse(f_ref[at, :]))
        r1_ref[:, at] = lay(inverse(s_ref[at, :]))
        return carry

    lax.fori_loop(0, total // block, norms, 0)
    r0 = r0_ref[...]
    r1 = r1_ref[...]
    sum_ref[...] = jnp.zeros_like(sum_ref)

    def column_sums(i, carry):
        at = pl.ds(pl.multiple_of(i * block, block), block)
        rows = s_ref[at, :]
        logit = dot(rows, f_ref[...], ((1,), (1,))) * (inverse(rows) * top) * r0
        sum_ref[...] += jnp.sum(jnp.exp(logit - top), axis=0, keepdims=True)
        return carry

    lax.fori_loop(0, total // block, column_sums, 0)
    lse_row = jnp.log(sum_ref[...]) + top
    first = f_ref[...]
    second = s_ref[...]
    first_own = f_ref[0:own, :]
    second_own = s_ref[0:own, :]
    r0_own = inverse(first_own)
    r1_own = inverse(second_own)
    eye = (
        lax.broadcasted_iota(jnp.int32, (own, total), 0)
        == lax.broadcasted_iota(jnp.int32, (own, total), 1)
    ).astype(F32)
    factor = scale_ref[0, 0] * (top / total)
    row_dots = dot(first_own, second, ((1,), (1,)))
    row_cos = row_dots * r0_own * r1
    row_logit = row_cos * top
    lse_own = jnp.log(jnp.sum(jnp.exp(row_logit - top), axis=-1, keepdims=True)) + top
    loss = (
        jnp.sum(lse_own - jnp.sum(eye * row_logit, axis=-1, keepdims=True), axis=0, keepdims=True)
        / total
    )
    align = (
        jnp.sum(
            2.0 - 2.0 * jnp.sum(eye * row_cos, axis=-1, keepdims=True), axis=0, keepdims=True
        )
        / total
    )
    self_cos = dot(first_own, first, ((1,), (1,))) * r0_own * r0
    unif = jnp.sum(
        jnp.sum(jnp.exp(4.0 * self_cos - 4.0), axis=-1, keepdims=True), axis=0, keepdims=True
    ) / (total * total)
    row_cg = factor * (jnp.exp(row_logit - lse_own) - eye)
    row_dd = (row_cg * r0_own * r1).astype(BF)
    e0 = jnp.sum(row_cg * row_dots * r1, axis=-1, keepdims=True)
    grad0 = dot(row_dd, second) - (e0 * r0_own * r0_own * r0_own) * first_own.astype(F32)
    col_dots = dot(second_own, first, ((1,), (1,)))
    col_cg = factor * (jnp.exp(col_dots * r1_own * r0 * top - lse_row) - eye)
    col_dd = (col_cg * r1_own * r0).astype(BF)
    e1 = jnp.sum(col_cg * col_dots * r0, axis=-1, keepdims=True)
    grad1 = dot(col_dd, first) - (e1 * r1_own * r1_own * r1_own) * second_own.astype(F32)
    bias = jnp.zeros((1, width), F32)
    for v, grad in enumerate((grad0, grad1)):
        pooled = pooled_ref[v * own : (v + 1) * own, :]
        pre = (grad * (1.0 - pooled * pooled)).astype(BF)
        pg_ref[v * own : (v + 1) * own, :] = pre
        bias = bias + jnp.sum(pre.astype(F32), axis=0, keepdims=True)
        back = dot(pre, pw_ref[...], ((1,), (1,)))
        high = back.astype(BF)
        hl_ref[2 * v * own : (2 * v + 1) * own, :] = high
        hl_ref[(2 * v + 1) * own : (2 * v + 2) * own, :] = (back - high.astype(F32)).astype(BF)
    pb_ref[...] = bias
    lane = lax.broadcasted_iota(jnp.int32, (1, 128), 1)
    sc_ref[...] = jnp.where(
        lane == 0, loss, jnp.where(lane == 1, align, jnp.where(lane == 2, unif, 0.0))
    )


def contrast(z, other, pooled, pooler_weight, loss_scale):
    own = pooled.shape[0] // 2
    total = z.shape[0]
    width = z.shape[1]
    block = min(512, total)
    vmem = pl.BlockSpec(memory_space=pltpu.VMEM)
    return pl.pallas_call(
        functools.partial(contrast_kernel, own, block),
        in_specs=[vmem, vmem, vmem, vmem, pl.BlockSpec(memory_space=pltpu.SMEM)],
        out_specs=[vmem] * 4,
        out_shape=[
            jax.ShapeDtypeStruct((2 * own, width), BF),
            jax.ShapeDtypeStruct((1, width), F32),
            jax.ShapeDtypeStruct((4 * own, width), BF),
            jax.ShapeDtypeStruct((1, 128), F32),
        ],
        scratch_shapes=[
            pltpu.VMEM((total, width), BF),
            pltpu.VMEM((total, width), BF),
            pltpu.VMEM((1, total), F32),
            pltpu.VMEM((1, total), F32),
            pltpu.VMEM((1, total), F32),
        ],
        cost_estimate=pl.CostEstimate(
            flops=2 * total * total * width, bytes_accessed=8 * total * width, transcendentals=0
        ),
        name="contrast",
    )(z, other, pooled, pooler_weight, loss_scale.reshape(1, 1))


def swap(x, axis, bit, size):
    return lax.ppermute(x, axis, [(i, i ^ bit) for i in range(size)])


def block_order(order, dp_size, rows):
    bits = len(order)
    index = lax.axis_index("dp")
    spot = jnp.arange(dp_size * rows, dtype=jnp.int32)
    place = spot // rows
    block = jnp.zeros_like(place)
    for stage, bit in enumerate(order):
        agrees = (place >> (bits - 1 - stage)) & 1
        block = block | ((((index >> bit) & 1) ^ 1 ^ agrees) << bit)
    source = block * rows + spot % rows
    return (lax.broadcasted_iota(jnp.int32, (spot.size, spot.size), 0) == source[None, :]).astype(BF)


def scatter_rows(triples, order, dp_size):
    half = triples[0][0].shape[1] // 2
    sent = [
        (dot(a[:, :half], b, ((0,), (0,))) + c[:half].astype(F32)).astype(BF)
        for a, b, c in triples
    ]
    kept = [
        (dot(a[:, half:], b, ((0,), (0,))) + c[half:].astype(F32)).astype(BF)
        for a, b, c in triples
    ]
    for stage, bit in enumerate(order):
        sent = sent[0] if len(sent) == 1 else jnp.concatenate(sent, axis=1)
        got = swap(sent, "dp", 1 << bit, dp_size)
        half //= 2
        sent, left = [], []
        at = 0
        for part in kept:
            mine = got[:, at : at + part.shape[1]]
            at += part.shape[1]
            if stage == len(order) - 1:
                left.append(part.astype(F32) + mine.astype(F32))
            else:
                sent.append((part[:half].astype(F32) + mine[:half].astype(F32)).astype(BF))
                left.append((part[half:].astype(F32) + mine[half:].astype(F32)).astype(BF))
        kept = left
    return kept


def pack_kernel(plan, which_ref, *refs):
    out_ref = refs[-1]
    out_ref[...] = jnp.zeros_like(out_ref)
    for ref, (kind, at) in zip(refs, plan):
        if kind == "row":
            size = ref.shape[1]
            out_ref[0:1, at : at + size] = ref[...]
        else:
            own, other, lo, hi = kind
            size = hi - lo
            first = which_ref[0] == 0
            a = refs[own][0:1, lo:hi]
            b = refs[other][0:1, lo:hi]
            out_ref[0:1, at : at + size] = jnp.where(first, a, b)
            out_ref[0:1, at + size : at + 2 * size] = jnp.where(first, b, a)


def on_device(
    dp_size,
    tokens,
    segments,
    cls_pos,
    keep_mask,
    cotangent,
    contrast_loss_scale,
    q_weight,
    q_bias,
    k_weight,
    v_weight,
    v_bias,
    o_weight,
    o_bias,
    norm1_gain,
    norm1_shift,
    up_weight,
    up_bias,
    down_weight,
    down_bias,
    norm2_gain,
    norm2_shift,
    pooler_weight,
    pool_bias,
):
    row_count, length, width = tokens.shape
    assert row_count == 1
    mp_index = lax.axis_index("mp")
    bits = dp_size.bit_length() - 1
    part = q_weight.shape[1]
    hidden = up_weight.shape[1]

    def partner(x):
        return lax.ppermute(x, "mp", [(0, 1), (1, 0)])

    biases = partner(jnp.concatenate([q_bias, v_bias, up_bias]))
    wq = (q_weight, partner(q_weight))
    wk = (k_weight, partner(k_weight))
    wv = (v_weight, partner(v_weight))
    wo = (o_weight, partner(o_weight))
    wu = (up_weight, partner(up_weight))
    wd = (down_weight, partner(down_weight))
    bq = (q_bias, biases[:part])
    bv = (v_bias, biases[part : 2 * part])
    bu = (up_bias, biases[2 * part :])

    rest = tuple(range(3, bits))
    xyz = (0, 1, 2) + rest
    yxz = (1, 0, 2) + rest
    by_x = block_order(xyz, dp_size, width // dp_size)
    by_y = block_order(yxz, dp_size, width // dp_size)
    tok = tokens[0]
    tok_x = dot(tok, by_x, out=BF)
    tok_y = dot(tok, by_y, out=BF)
    seg = lax.dynamic_slice(segments[0], (mp_index * length,), (length,))
    seg_col = seg[:, None]
    seg_win = jnp.stack([seg[w : w + WIN] for _, w in windows(length)])
    keep = keep_mask[0].transpose(1, 2, 0, 3).astype(BF)
    cot = cotangent[0].transpose(1, 0, 2)

    qs, ks, vs, mixed = [], [], [], []
    for h in range(2):
        q, k, v, o = attend(tok, wq[h], wk[h], wv[h], bq[h], bv[h], seg_col, seg_win)
        qs.append(q)
        ks.append(k)
        vs.append(v)
        mixed.append(o)
    attn = dot(mixed[0], wo[0]) + dot(mixed[1], wo[1]) + o_bias
    tok32 = tok.astype(F32)
    pre1 = tok32[None] + keep[0].astype(F32) * KEEP_SCALE * attn[None]
    hid, hat1, inv1 = norm_forward(pre1, norm1_gain, norm1_shift)
    hid_low = hid.astype(BF).reshape(2 * length, width)
    hid_order = dot(hid_low, by_y, out=BF)
    gs, slopes = [], []
    for h in range(2):
        u = dot(hid_low, wu[h]) + bu[h]
        phi = 0.5 * (1.0 + lax.erf(u * INV_ROOT_TWO))
        gs.append((u * phi).astype(BF))
        slopes.append((phi + u * jnp.exp(-0.5 * u * u) * INV_ROOT_TWO_PI).astype(BF))
    down = dot(gs[0], wd[0]) + dot(gs[1], wd[1]) + down_bias
    pre2 = hid + keep[1].astype(F32) * KEEP_SCALE * down.reshape(2, length, width)
    out, hat2, inv2 = norm_forward(pre2, norm2_gain, norm2_shift)
    out_low = out.astype(BF)

    local_pos = cls_pos[0] - mp_index * length
    sent = local_pos.shape[0]
    picker = (local_pos[:, None] == jnp.arange(length, dtype=jnp.int32)[None, :]).astype(BF)
    pooled_in = jnp.concatenate([dot(picker, out_low[v], out=BF) for v in range(2)], axis=0)
    pooled = jnp.tanh(dot(pooled_in, pooler_weight) + pool_bias)
    z = pooled.astype(BF)
    for bit in reversed(range(bits)):
        other = swap(z, "dp", 1 << bit, dp_size)
        z = jnp.concatenate([z, other], axis=0)
    other = partner(z)
    pre_grad, pool_bias_grad, high_low, scalars = contrast(
        z, other, pooled, pooler_weight, contrast_loss_scale
    )
    picker2 = jnp.concatenate([picker, picker], axis=0)
    row_grad = jnp.stack(
        [dot(picker2, high_low[2 * v * sent : 2 * (v + 1) * sent], ((0,), (0,))) for v in range(2)]
    )

    dy = cot.astype(F32) + row_grad
    dr2, gain2_grad, shift2_grad = norm_backward(dy, hat2, inv2, norm2_gain)
    df = dr2 * (keep[1].astype(F32) * KEEP_SCALE)
    down_bias_grad = jnp.sum(df, axis=(0, 1))
    df_low = df.astype(BF).reshape(2 * length, width)

    def triple(left, right):
        sent = dot(left, right[1], ((0,), (0,)), BF)
        got = partner(sent)
        return left, right[0], got

    pool_own, pool_other = (
        lax.dynamic_slice(pooled_in, (0, which * part), (2 * sent, part))
        for which in (mp_index, 1 - mp_index)
    )
    df_order = dot(df_low, by_x, out=BF)
    pre_order = dot(pre_grad, by_x, out=BF)
    g_down, g_pool = scatter_rows(
        [triple(df_order, gs), triple(pre_order, (pool_own, pool_other))], xyz, dp_size
    )
    dus = []
    up_bias_grads = []
    for h in range(2):
        du = (dot(df_low, wd[h], ((1,), (1,))) * slopes[h].astype(F32)).astype(BF)
        up_bias_grads.append(jnp.sum(du.astype(F32), axis=0))
        dus.append(du)
    (g_up,) = scatter_rows([triple(hid_order, dus)], yxz, dp_size)
    dh = dot(dus[0], wu[0], ((1,), (1,))) + dot(dus[1], wu[1], ((1,), (1,)))
    dh = dr2 + dh.reshape(2, length, width)
    dr1, gain1_grad, shift1_grad = norm_backward(dh, hat1, inv1, norm1_gain)
    resid = dr1[0] + dr1[1]
    da = (dr1[0] * keep[0, 0].astype(F32) + dr1[1] * keep[0, 1].astype(F32)) * KEEP_SCALE
    o_bias_grad = jnp.sum(da, axis=0)
    da_low = da.astype(BF)
    o_triple = triple(dot(da_low, by_y, out=BF), mixed)
    joint, bias_sums = [None] * 2, [None] * 2
    for h in (1, 0):
        dmix = dot(da_low, wo[h], ((1,), (1,)), BF)
        joint[h], bias_sums[h] = attend_back(qs[h], ks[h], vs[h], dmix, seg_col, seg_win)
    two = 2 * part
    (g_qk,) = scatter_rows([triple(tok_x, [j[:, :two] for j in joint])], xyz, dp_size)
    g_q, g_k = g_qk[:, :part], g_qk[:, part:]
    g_v, g_o = scatter_rows([triple(tok_y, [j[:, two:] for j in joint]), o_triple], yxz, dp_size)
    tok_grad = resid
    for h in (1, 0):
        for i, w in enumerate((wq, wk, wv)):
            tok_grad = tok_grad + dot(joint[h][:, i * part : (i + 1) * part], w[h], ((1,), (1,)))

    rows = [
        gain1_grad,
        shift1_grad,
        o_bias_grad,
        gain2_grad,
        shift2_grad,
        down_bias_grad,
        pool_bias_grad,
        scalars,
    ]
    rows = [r.reshape(1, -1) for r in rows]
    halves = [r.reshape(1, -1) for r in bias_sums + up_bias_grads]
    spots = []
    plan = []
    at = 0
    for row in rows:
        plan.append(("row", at))
        spots.append((at, row.shape[1]))
        at += row.shape[1]
    first_half = len(rows)
    for own, lo, hi in (
        (first_half, 0, part),
        (first_half, part, 2 * part),
        (first_half + 2, 0, hidden),
    ):
        plan.append(((own, own + 1, lo, hi), at))
        spots.append((at, 2 * (hi - lo)))
        at += 2 * (hi - lo)
    vmem = pl.BlockSpec(memory_space=pltpu.VMEM)
    small = pl.pallas_call(
        functools.partial(pack_kernel, tuple(plan)),
        in_specs=[pl.BlockSpec(memory_space=pltpu.SMEM)] + [vmem] * (len(rows) + len(halves)),
        out_specs=vmem,
        out_shape=jax.ShapeDtypeStruct((1, at), F32),
        name="pack",
    )(mp_index.reshape(1).astype(jnp.int32), *rows, *halves)
    got = partner(small)
    small = small + got
    for bit in (3, 2, 0, 1) + tuple(range(4, bits)):
        got = swap(small, "dp", 1 << bit, dp_size)
        small = small + got
    outs = [small[0, lo : lo + size] for lo, size in spots]
    scalars = outs[7]
    outs = outs[:7] + outs[8:]
    return (
        scalars[0],
        out_low.transpose(1, 0, 2)[None],
        tok_grad[None],
        g_q,
        outs[7],
        g_k,
        g_v,
        outs[8],
        g_o.T,
        outs[2],
        outs[0],
        outs[1],
        g_up,
        outs[9],
        g_down.T,
        outs[5],
        outs[3],
        outs[4],
        g_pool.T,
        outs[6],
        scalars[1],
        jnp.log(scalars[2]),
    )


def solution(mesh):
    rep = P()
    in_specs = (
        P("dp", "mp", None),
        P("dp", None),
        P("dp", "mp"),
        P("dp", "mp", None, None, None),
        P("dp", "mp", None, None),
        rep,
        P(None, "mp"),
        P("mp"),
        P(None, "mp"),
        P(None, "mp"),
        P("mp"),
        P("mp", None),
        rep,
        rep,
        rep,
        P(None, "mp"),
        P("mp"),
        P("mp", None),
        rep,
        rep,
        rep,
        rep,
        rep,
    )
    out_specs = (
        rep,
        P("dp", "mp", None, None),
        P("dp", "mp", None),
        P("dp", "mp"),
        rep,
        P("dp", "mp"),
        P("dp", "mp"),
        rep,
        P("mp", "dp"),
        rep,
        rep,
        rep,
        P("dp", "mp"),
        rep,
        P("mp", "dp"),
        rep,
        rep,
        rep,
        P("mp", "dp"),
        rep,
        rep,
        rep,
    )

    def body(*args):
        return on_device(mesh.shape["dp"], *args)

    return jax.shard_map(body, mesh=mesh, in_specs=in_specs, out_specs=out_specs, check_vma=False)
```
